1024 devices in a mesh: grp: 4 (over y), seq: 32 (over x, z_lo), rep: 8 (over z_hi, core).
Axes of the slice: x: 4, y: 4, z: 32 (z_hi: 4, z_lo: 8; z = z_hi * 8 + z_lo), core: 2. Of those that a mesh axis runs over, the one named last changes fastest.
Arguments:
- query_rows: bfloat16 [8, 4, 4096, 2560], P('rep', 'grp', 'seq'), may hold values from -8 to 8
- key_rows: bfloat16 [8, 4, 4096, 2560], P('rep', 'grp', 'seq'), may hold values from -8 to 8
- value_rows: bfloat16 [8, 4, 4096, 2560], P('rep', 'grp', 'seq'), may hold values from -6 to 6
- view_frame: int32 [8, 4, 4096], P('rep', 'grp', 'seq'), may hold values from 0 to 39, never falling along the last dimension, each value on 1 to 128 neighbouring positions
- control_row: int32 [8, 4, 4096], P('rep', 'grp', 'seq'), may hold values from 0 to 4095, as said below
- control_gate: float32 [2560], P('rep'), may hold values from 0.2 to 1.6
- out_grad: bfloat16 [8, 4, 4096, 2560], P('rep', 'grp', 'seq'), may hold values from -6 to 6
Outputs:
- block_out: bfloat16 [8, 4, 4096, 2560], P('rep', 'grp', 'seq')
- branch_grad: bfloat16 [8, 4096, 2560], P('rep', 'seq')
The draws below stay inside these ranges and needn't reach their ends.
Inputs may be any that keep to these rules, and one draw needn't show every extreme that they name: `view_frame`: values never fall along a sequence; value // 20 is the camera and value % 20 the frame; one value holds at most 128 positions. `control_row`: position t of a sequence takes a row r with r // 128 == t // 128.
All inputs are finite; a program needn't handle non-finite values.
Results may differ from the reference program's by a relative error of at most 0.0057.
Values may be sent and summed in bfloat16 or wider, within the bound.
A program may use at most 64 MiB of HBM per device.

```python
import math
import jax
import jax.numpy as jnp
import numpy as np
from jax import lax

HEADS = 32
DH = 80
TOK_DEV = 128
FRAMES = 20
SEGS = 40
L = 4096
FRAME_MOST = 128
REACH = 256
BLOCK = 512
HD = 2560
CLIPS = 8
GROUPS = 4


def paired_rows(key):
    base = jax.random.fold_in(key, 7)
    first, second = jax.random.split(base, 2)
    shape = (CLIPS, GROUPS, L, HEADS * DH)
    queries = jnp.clip(jax.random.normal(first, shape, jnp.float32), -6.0, 6.0)
    keys_out = jnp.clip(jax.random.normal(second, shape, jnp.float32), -6.0, 6.0)
    return (queries, keys_out)


def draw_query_rows(key, part):
    return paired_rows(key)[0].astype(jnp.bfloat16)


def draw_key_rows(key, part):
    return paired_rows(key)[1].astype(jnp.bfloat16)


def draw_control_row(key, part):
    base = jax.random.fold_in(key, 11)
    first, second, third = jax.random.split(base, 3)
    blocks_count = L // TOK_DEV
    shape = (CLIPS, GROUPS, blocks_count, TOK_DEV)
    side_shape = (CLIPS, GROUPS, blocks_count, 1)
    rows_out = jax.random.randint(first, shape, 0, TOK_DEV)
    top_place = jax.random.randint(second, side_shape, 0, TOK_DEV)
    low_place = (top_place + 1 + jax.random.randint(third, side_shape, 0, TOK_DEV - 1)) % TOK_DEV
    places = jnp.arange(TOK_DEV, dtype=jnp.int32)
    rows_out = jnp.where(places == top_place, TOK_DEV - 1, rows_out)
    rows_out = jnp.where(places == low_place, 0, rows_out)
    offsets = (jnp.arange(blocks_count, dtype=jnp.int32) * TOK_DEV)[:, None]
    rows_out = rows_out + offsets
    return rows_out.reshape(CLIPS, GROUPS, L).astype(jnp.int32)


def block_levels(stream_key, extent, cuts, smallest, high):
    gain = 1.0
    for dim, blocks in cuts:
        heights = jax.random.uniform(jax.random.fold_in(jax.random.fold_in(stream_key, 6), dim), (blocks,), jnp.float32, smallest / len(cuts), high / len(cuts))
        gain = gain * jnp.repeat(jnp.exp(heights), extent[dim] // blocks).reshape((-1,) + (1,) * (len(extent) - 1 - dim))
    return gain


def split_up(number_of, total, bound, skew):
    portions = [(1 << 20) // math.isqrt(standing ** skew) + 1 for standing in range(2, number_of + 1)]
    rest, holding = total - bound - (number_of - 1), [1] * (number_of - 1)
    while rest > 0:
        movable = [i for i in range(number_of - 1) if holding[i] < bound]
        pool, remaining = sum([portions[i] for i in movable]), rest
        for i in movable:
            more = min(bound - holding[i], max(1, remaining * portions[i] // pool), rest)
            holding[i] = holding[i] + more
            rest = rest - more
    return np.array([bound] + holding)


def uneven(own_key, count, total, limit, skew):
    if count == 2:
        one = jax.random.randint(own_key, (), max(1, total - limit), min(limit, total - 1) + 1)
        return jnp.stack([one, total - one])
    lengths = jnp.asarray(split_up(count, total, limit, skew), jnp.int32)
    couples = (count - 1) // 2
    giver, taker = lengths[1:1 + 2 * couples:2], lengths[2:2 + 2 * couples:2]
    margin = jnp.minimum(giver - 1, limit - taker)
    shifted = jax.random.randint(jax.random.fold_in(own_key, 1), (couples,), 0, 1 << 20) % (margin + 1)
    lengths = lengths.at[1:1 + 2 * couples:2].set(giver - shifted).at[2:2 + 2 * couples:2].set(taker + shifted)
    return lengths[jax.random.permutation(jax.random.fold_in(own_key, 2), count)]


def noise(own_key, extent, spread, bound, cuts=(), kind=jnp.bfloat16):
    factor_of = block_levels(own_key, extent, cuts, -0.22, 0.18) if cuts else 1.0
    values = jax.random.normal(own_key, extent, jnp.float32) * spread * factor_of
    return jnp.minimum(jnp.maximum(values, -bound), bound).astype(kind)


def setup_inputs(seed: int = 0) -> dict:
    arg_keys = jax.random.split(jax.random.key(seed), 8)
    query_rows = draw_query_rows(jax.random.fold_in(arg_keys[7], 71), 0)
    key_rows = draw_key_rows(jax.random.fold_in(arg_keys[7], 71), 0)
    value_rows = noise(arg_keys[2], (CLIPS, GROUPS, L, HD), 1.0, 6.0, ((0, 8), (1, 4), (2, 32)))
    view_frame = jax.vmap(lambda own: jnp.searchsorted(jnp.cumsum(uneven(own, SEGS, L, FRAME_MOST, 1)), jnp.arange(L), side="right"))(jax.random.split(arg_keys[3], CLIPS * GROUPS)).reshape((CLIPS, GROUPS, L)).astype(jnp.int32)
    control_row = draw_control_row(jax.random.fold_in(arg_keys[7], 71), 0)
    control_gate = jnp.clip(0.2 + 1.4 * jax.random.uniform(arg_keys[5], (HD,), jnp.float32) ** block_levels(arg_keys[5], (HD,), ((0, 8),), -0.2, 0.2), 0.2, 1.6)
    out_grad = noise(arg_keys[6], (CLIPS, GROUPS, L, HD), 1.0, 6.0, ((0, 8), (1, 4), (2, 32)))
    return {"query_rows": query_rows, "key_rows": key_rows, "value_rows": value_rows, "view_frame": view_frame, "control_row": control_row, "control_gate": control_gate, "out_grad": out_grad}


def attend(queries, keys_pad, values_pad, query_tag, key_tag, reach_rows, frame_count, block_rows):
    length = queries.shape[-1]
    window = block_rows + 2 * reach_rows
    factor = 1.0 / math.sqrt(queries.shape[1])

    def one_block(block_index):
        first_row = block_index * block_rows
        query_block = lax.dynamic_slice_in_dim(queries, first_row, block_rows, 2).astype(jnp.float32)
        key_block = lax.dynamic_slice_in_dim(keys_pad, first_row, window, 2).astype(jnp.float32)
        value_block = lax.dynamic_slice_in_dim(values_pad, first_row, window, 2).astype(jnp.float32)
        query_seg = lax.dynamic_slice_in_dim(query_tag, first_row, block_rows, 0) - 1
        key_seg = lax.dynamic_slice_in_dim(key_tag, first_row, window, 0) - 1
        allowed = (key_seg[None, :] >= 0) & (query_seg[:, None] // frame_count == key_seg[None, :] // frame_count) & (jnp.abs(query_seg[:, None] - key_seg[None, :]) <= 1)
        scores = jnp.einsum('hdq,hdk->hqk', query_block, key_block) * factor
        scores = jnp.where(allowed[None], scores, -1e+30)
        largest = lax.optimization_barrier(jnp.max(scores, axis=-1, keepdims=True))
        powers = jnp.exp(scores - largest)
        totals = lax.optimization_barrier(jnp.sum(powers, axis=-1, keepdims=True))
        weights = (powers / totals).astype(jnp.bfloat16)
        mixed_rows = jnp.einsum('hqk,hdk->hdq', weights.astype(jnp.float32), value_block)
        return mixed_rows.astype(jnp.bfloat16)
    blocks = lax.map(one_block, jnp.arange(length // block_rows, dtype=jnp.int32))
    heads_count = queries.shape[0]
    return jnp.moveaxis(blocks, 0, 2).reshape(heads_count, queries.shape[1], length)

def reference(query_rows, key_rows, value_rows, view_frame, control_row, control_gate, out_grad):
    tags = (view_frame + 1).astype(jnp.int32)
    pad_rows = ((0, 0), (0, 0), (REACH, REACH))

    def head_major(rows_in):
        return rows_in.reshape(L, HEADS, DH).transpose(1, 2, 0)

    def one_sequence(packed):
        queries, keys_in, values_in, query_tag = packed
        keys_pad = jnp.pad(head_major(keys_in), pad_rows)
        values_pad = jnp.pad(head_major(values_in), pad_rows)
        key_tag = jnp.pad(query_tag, (REACH, REACH))
        result = attend(head_major(queries), keys_pad, values_pad, query_tag, key_tag, REACH, FRAMES, BLOCK)
        return result.transpose(2, 0, 1).reshape(L, HEADS * DH)

    def flatten_groups(array):
        return array.reshape((CLIPS * GROUPS,) + array.shape[2:])
    attended = lax.map(one_sequence, (flatten_groups(query_rows), flatten_groups(key_rows), flatten_groups(value_rows), flatten_groups(tags)))
    attended = attended.reshape(CLIPS, GROUPS, L, HEADS * DH)
    branch_rows = attended[:, 0]
    relayed = jax.vmap(lambda rows_in, picks: rows_in[picks])(branch_rows, control_row)
    block_out = (attended.astype(jnp.float32) + control_gate * relayed.astype(jnp.float32)).astype(jnp.bfloat16)

    def gathered_grad(grads, picks):
        flat_grads = grads.reshape(-1, HEADS * DH).astype(jnp.float32)
        return jax.ops.segment_sum(flat_grads, picks.reshape(-1), num_segments=L)
    summed = jax.vmap(gathered_grad)(out_grad, control_row)
    branch_grad = (out_grad[:, 0].astype(jnp.float32) + control_gate * summed).astype(jnp.bfloat16)
    return (block_out, branch_grad)
```

```python
import functools
import math

import jax
import jax.numpy as jnp
from jax import lax
from jax.experimental import pallas as pl
from jax.experimental.pallas import tpu as pltpu
from jax.sharding import PartitionSpec as P

DH = 80
LANES = 128
CHUNK = 640
HEADS_CHUNK = CHUNK // DH
PARTS = (
    (range(0, 5), (0, 384)),
    (range(5, 8), (384, 256)),
)
RUN = 8
QUARTER = 32
ROWS = 128
WINDOW = 5 * ROWS
ABSENT = -1000
MESH = pl.DeviceIdType.MESH
SCALE = math.log2(math.e) / math.sqrt(DH)
OWN, LOWER, UPPER = 2, (1, 0), (3, 4)


def head_spans(head):
    first, last = head * DH, head * DH + DH
    spans = []
    for block in range(first // LANES, (last + LANES - 1) // LANES):
        low = max(first - block * LANES, 0)
        high = min(last - block * LANES, LANES)
        spans.append((block, low, high))
    return spans


def kernel(
    chunks,
    q_hbm,
    k_hbm,
    v_hbm,
    tag_ref,
    ctrl_ref,
    gate_ref,
    grad_hbm,
    out_ref,
    bgrad_ref,
    q_buf,
    k_win,
    v_win,
    tags,
    ctrls,
    gates,
    grads,
    bias,
    select,
    bounce,
    carry_buf,
    attended,
    branch,
    kv_send,
    kv_recv,
    cross_send,
    bounce_recv,
    pass_send,
    tag_send,
    tag_recv,
    gate_send,
    gate_recv,
    grad_send,
    grad_recv,
    ctrl_send,
    ctrl_recv,
    br_send,
    br_recv,
    local_sem,
):
    p = lax.axis_index("seq")
    grp = lax.axis_index("grp")
    rep = lax.axis_index("rep")
    length = lax.axis_size("seq")
    groups = lax.axis_size("grp")
    core, far = rep % 2, rep // 2
    n_far = lax.axis_size("rep") // 2
    far_up, far_down, far_two = (far + 1) % n_far, (far + n_far - 1) % n_far, (far + 2) % n_far
    sibling = far * 2 + 1 - core
    has_low, has_high = p >= 1, p <= length - 2
    inner = has_low & has_high
    low2, high2 = p >= 2, p <= length - 3
    place, column, n_columns = p % RUN, p // RUN, length // RUN
    first, last, second, late = place == 0, place == RUN - 1, place == 1, place == RUN - 2
    edge, side = first | last, first | last | second | late
    left, right = column >= 1, column <= n_columns - 2
    side_left, side_right = side & left, side & right
    crosses = (
        (last & right, late & right),
        (first & left, second & left),
    )
    through = (column + 1, n_columns - column)
    passes = ((last & left, late & left), (first & right, second & right))
    passed = (column, n_columns - 1 - column)
    relays = (inner & ~last, inner & ~first)

    barrier = pltpu.get_barrier_semaphore()

    def greet(**where):
        pl.semaphore_signal(barrier, inc=1, device_id=where, device_id_type=MESH)

    @pl.when(has_low)
    def _():
        greet(seq=p - 1)

    @pl.when(has_high)
    def _():
        greet(seq=p + 1)

    @pl.when(low2)
    def _():
        greet(seq=p - 2)

    @pl.when(high2)
    def _():
        greet(seq=p + 2)

    for there, distance in (
        (first, RUN - 1),
        (last, 1 - RUN),
        (first | second, RUN - 2),
        (last | late, 2 - RUN),
        (side_left, -RUN),
        (side_right, RUN),
    ):

        @pl.when(there)
        def _(distance=distance):
            greet(seq=p + distance)

    for step in range(1, groups):
        greet(grp=(grp + step) % groups)
    greet(rep=sibling)
    greet(rep=far_up * 2 + core)
    greet(rep=far_down * 2 + core)
    near = groups - 1 + 3

    own_rows = pl.ds(OWN * ROWS, ROWS)
    locals_ = [
        pltpu.make_async_copy(q_hbm, q_buf, local_sem.at[0]),
        pltpu.make_async_copy(k_hbm, k_win.at[own_rows, :], local_sem.at[1]),
        pltpu.make_async_copy(v_hbm, v_win.at[own_rows, :], local_sem.at[2]),
        pltpu.make_async_copy(grad_hbm, grads.at[grp], local_sem.at[3]),
        pltpu.make_async_copy(ctrl_ref, ctrls.at[grp], local_sem.at[4]),
        pltpu.make_async_copy(gate_ref, gates.at[core, far], local_sem.at[5]),
        pltpu.make_async_copy(tag_ref, tags.at[OWN], local_sem.at[6]),
    ]
    for copy in locals_:
        copy.start()

    def fill(block):
        rows = pl.ds(block * ROWS, ROWS)
        k_win[rows, :] = jnp.zeros((ROWS, k_win.shape[1]), k_win.dtype)
        v_win[rows, :] = jnp.zeros((ROWS, v_win.shape[1]), v_win.dtype)
        tags[block] = jnp.full((1, ROWS), ABSENT, jnp.int32)

    for absent, block in (
        (~has_low, LOWER[0]),
        (~low2, LOWER[1]),
        (~has_high, UPPER[0]),
        (~high2, UPPER[1]),
    ):

        @pl.when(absent)
        def _(block=block):
            fill(block)

    peers = near
    for there in (has_low, has_high, low2, high2, edge, side, side_left, side_right):
        peers = peers + there.astype(jnp.int32)
    pl.semaphore_wait(barrier, peers)

    def columns(chunk, span=(0, CHUNK)):
        start = chunk * CHUNK + span[0]
        if not isinstance(start, int):
            start = pl.multiple_of(start, LANES)
        return pl.ds(start, span[1])

    def kv_copy(way, hop, chunk, part):
        cols = columns(chunk)
        land = (LOWER, UPPER)[way]
        win, hbm = ((k_win, k_hbm), (v_win, v_hbm))[part]
        source = hbm.at[:, cols] if hop == 0 else win.at[pl.ds(land[0] * ROWS, ROWS), cols]
        return pltpu.make_async_remote_copy(
            src_ref=source,
            dst_ref=win.at[pl.ds(land[hop] * ROWS, ROWS), cols],
            send_sem=kv_send.at[way, hop, chunk, part],
            recv_sem=kv_recv.at[way, hop, chunk, part, 0],
            device_id={"seq": p + (1, -1)[way]},
            device_id_type=MESH,
        )

    def cross_copy(way, hop, chunk, part, piece, detour):
        cols = columns(chunk)
        rows = pl.ds(piece * QUARTER, QUARTER)
        if detour:
            target = bounce.at[part, rows, cols]
            arrived, where = bounce_recv.at[chunk, part, piece], p + (RUN, -RUN)[way]
        else:
            block = (LOWER, UPPER)[way][hop]
            target = (k_win, v_win)[part].at[pl.ds(block * ROWS + piece * QUARTER, QUARTER), cols]
            arrived = kv_recv.at[way, hop, chunk, part, piece]
            where = p + (hop + 1, -hop - 1)[way]
        return pltpu.make_async_remote_copy(
            src_ref=(k_hbm, v_hbm)[part].at[rows, cols],
            dst_ref=target,
            send_sem=cross_send.at[chunk, part, piece],
            recv_sem=arrived,
            device_id={"seq": where},
            device_id_type=MESH,
        )

    def pass_copy(way, hop, chunk, part, piece):
        cols = columns(chunk)
        block = (LOWER, UPPER)[way][hop]
        rows = pl.ds(block * ROWS + piece * QUARTER, QUARTER)
        return pltpu.make_async_remote_copy(
            src_ref=bounce.at[part, pl.ds(piece * QUARTER, QUARTER), cols],
            dst_ref=(k_win, v_win)[part].at[rows, cols],
            send_sem=pass_send.at[chunk, part, piece],
            recv_sem=kv_recv.at[way, hop, chunk, part, piece],
            device_id={"seq": p + (1 + hop - RUN, RUN - 1 - hop)[way]},
            device_id_type=MESH,
        )

    def tag_copy(way, hop):
        return pltpu.make_async_remote_copy(
            src_ref=tag_ref,
            dst_ref=tags.at[(LOWER, UPPER)[way][hop]],
            send_sem=tag_send.at[way, hop],
            recv_sem=tag_recv.at[way, hop],
            device_id={"seq": p + (hop + 1, -hop - 1)[way]},
            device_id_type=MESH,
        )

    tag_sends = ((0, 0, has_high), (0, 1, high2), (1, 0, has_low), (1, 1, low2))
    tag_arrivals = ((0, 0, has_low), (0, 1, low2), (1, 0, has_high), (1, 1, high2))

    def on_crossing(chunk, act):
        for way in range(2):
            for hop in range(2):
                for piece in range(4):
                    direct = piece >= through[way]

                    @pl.when(crosses[way][hop] & direct)
                    def _(way=way, hop=hop, piece=piece):
                        for part in range(2):
                            act(cross_copy(way, hop, chunk, part, piece, False))

                    if piece < 3:

                        @pl.when(crosses[way][hop] & ~direct)
                        def _(way=way, hop=hop, piece=piece):
                            for part in range(2):
                                act(cross_copy(way, hop, chunk, part, piece, True))

    def on_own(chunk, act):
        for way, there in ((0, has_high & ~last), (1, has_low & ~first)):

            @pl.when(there)
            def _(way=way):
                for part in range(2):
                    act(kv_copy(way, 0, chunk, part))

    def on_relay(chunk, act):
        for way in range(2):

            @pl.when(relays[way])
            def _(way=way):
                for part in range(2):
                    act(kv_copy(way, 1, chunk, part))

    def on_arrival(way, hop, chunk):
        in_edge = (first, last)[way]

        @pl.when(~in_edge)
        def _():
            for part in range(2):
                kv_copy(way, hop, chunk, part).wait_recv()

        @pl.when(in_edge)
        def _():
            for piece in range(4):
                for part in range(2):
                    cross_copy(way, hop, chunk, part, piece, False).wait_recv()

    def start(copy):
        copy.start()

    def left_(copy):
        copy.wait_send()

    def own_send(chunk):
        on_crossing(chunk, start)
        on_own(chunk, start)

    def relay(chunk):
        for way, here in ((0, has_low), (1, has_high)):

            @pl.when(here)
            def _(way=way):
                on_arrival(way, 0, chunk)

        on_relay(chunk, start)

    def arrive(chunk):
        for way, here in ((0, low2), (1, high2)):

            @pl.when(here)
            def _(way=way):
                on_arrival(way, 1, chunk)

    def on_pass(chunk, act):
        for way in range(2):
            for hop in range(2):
                for piece in range(3):

                    @pl.when(passes[way][hop] & (piece < passed[way]))
                    def _(way=way, hop=hop, piece=piece):
                        for part in range(2):
                            act(way, hop, chunk, part, piece)

    def forward(way, hop, chunk, part, piece):
        cross_copy(way, hop, chunk, part, piece, True).wait_recv()
        pass_copy(way, hop, chunk, part, piece).start()

    def forwarded(way, hop, chunk, part, piece):
        pass_copy(way, hop, chunk, part, piece).wait_send()

    def gate_copy(piece, target, slot, source=None):
        return pltpu.make_async_remote_copy(
            src_ref=gates.at[core, piece] if source is None else source,
            dst_ref=gates.at[core, piece],
            send_sem=gate_send.at[slot],
            recv_sem=gate_recv.at[core, piece],
            device_id={"rep": target},
            device_id_type=MESH,
        )

    to_up, to_down = far_up * 2 + core, far_down * 2 + core
    gate_copies = [
        gate_copy(far, to_up, 0, gate_ref),
        gate_copy(far, to_down, 1, gate_ref),
        gate_copy(far, sibling, 2, gate_ref),
        gate_copy(far_down, to_up, 3),
        gate_copy(far_down, sibling, 4),
        gate_copy(far_up, sibling, 5),
        gate_copy(far_two, sibling, 6),
    ]

    def gate_arrival(which, piece):
        return pltpu.make_async_remote_copy(
            src_ref=gate_ref,
            dst_ref=gates.at[which, piece],
            send_sem=gate_send.at[0],
            recv_sem=gate_recv.at[which, piece],
            device_id={"rep": sibling},
            device_id_type=MESH,
        )

    def grad_copy(step):
        return pltpu.make_async_remote_copy(
            src_ref=grad_hbm,
            dst_ref=grads.at[grp],
            send_sem=grad_send.at[step - 1],
            recv_sem=grad_recv.at[grp],
            device_id={"grp": (grp + step) % groups},
            device_id_type=MESH,
        )

    def ctrl_copy(step):
        return pltpu.make_async_remote_copy(
            src_ref=ctrl_ref,
            dst_ref=ctrls.at[grp],
            send_sem=ctrl_send.at[step - 1],
            recv_sem=ctrl_recv.at[grp],
            device_id={"grp": (grp + step) % groups},
            device_id_type=MESH,
        )

    def grad_arrival(step):
        source = (grp + step) % groups
        for src, dst, sem in ((grad_hbm, grads, grad_recv), (ctrl_ref, ctrls, ctrl_recv)):
            pltpu.make_async_remote_copy(
                src_ref=src,
                dst_ref=dst.at[source],
                send_sem=grad_send.at[0],
                recv_sem=sem.at[source],
                device_id={"grp": source},
                device_id_type=MESH,
            ).wait_recv()

    def branch_copy(chunk, half, step):
        cols = columns(chunk, PARTS[half][1])
        return pltpu.make_async_remote_copy(
            src_ref=branch.at[:, cols],
            dst_ref=branch.at[:, cols],
            send_sem=br_send.at[chunk, half, step - 1],
            recv_sem=br_recv.at[chunk, half],
            device_id={"grp": step},
            device_id_type=MESH,
        )

    for way, hop, there in tag_sends:

        @pl.when(there)
        def _(way=way, hop=hop):
            tag_copy(way, hop).start()

    for copy in gate_copies[:3]:
        copy.start()
    own_send(0)
    own_send(1)
    for step in range(1, groups):
        ctrl_copy(step).start()
        grad_copy(step).start()
    for copy in locals_:
        copy.wait()
    gate_arrival(core, far_down).wait_recv()
    gate_copies[3].start()
    gate_copies[4].start()
    gate_arrival(core, far_up).wait_recv()
    gate_copies[5].start()
    for chunk in range(2, chunks):
        own_send(chunk)

    for way, hop, here in tag_arrivals:

        @pl.when(here)
        def _(way=way, hop=hop):
            tag_copy(way, hop).wait_recv()

    def column_of(row):
        return jnp.broadcast_to(row.astype(jnp.float32), (ROWS, ROWS)).T

    query_tag = column_of(tags[OWN])
    for block in range(5):
        key_tag = jnp.broadcast_to(tags[block].astype(jnp.float32), (ROWS, ROWS))
        gap = jnp.abs(query_tag - key_tag)
        camera = (query_tag >= 20.0) == (key_tag >= 20.0)
        bias[:, block * ROWS : (block + 1) * ROWS] = jnp.where((gap <= 1.0) & camera, 0.0, -1e30)

    def selector(which):
        rows = lax.broadcasted_iota(jnp.int32, (ROWS, ROWS), 0)
        return jnp.where(rows == jnp.broadcast_to(ctrls[which] % ROWS, (ROWS, ROWS)), 1.0, 0.0)

    select[...] = selector(grp).T.astype(jnp.bfloat16)

    lane = lax.broadcasted_iota(jnp.int32, (ROWS, LANES), 1)

    def compute(chunk, half):
        def cols(block, count=1):
            return pl.ds(pl.multiple_of(chunk * CHUNK + block * LANES, LANES), count * LANES)

        heads, (result_first, result_width) = PARTS[half]
        pending = {}
        if half == 1:
            pending[result_first // LANES] = carry_buf[...]
        for head in heads:
            spans = head_spans(head)
            width = len(spans)
            queries = []
            for block, low, high in spans:
                part = q_buf[:, cols(block)]
                if (low, high) != (0, LANES):
                    part = jnp.where((lane >= low) & (lane < high), part, jnp.zeros_like(part))
                queries.append(part)
            query = queries[0] if width == 1 else jnp.concatenate(queries, axis=1)
            where = cols(spans[0][0], width)
            scores = lax.dot_general(
                query, k_win[:, where], (((1,), (1,)), ((), ())), preferred_element_type=jnp.float32
            )
            scores = scores + bias[...]
            largest = jnp.max(scores, axis=1, keepdims=True)
            powers = jnp.exp2((scores - largest) * SCALE)
            totals = jnp.sum(powers, axis=1, keepdims=True)
            weights = (powers * (1.0 / totals)).astype(jnp.bfloat16)
            mixed = jnp.dot(weights, v_win[:, where], preferred_element_type=jnp.float32)
            for number, (block, low, high) in enumerate(spans):
                piece = mixed[:, number * LANES : (number + 1) * LANES]
                if block in pending:
                    piece = jnp.where(lane >= low, piece, pending[block])
                if high == LANES:
                    pending.pop(block, None)
                    attended[:, cols(block)] = piece.astype(jnp.bfloat16)
                else:
                    pending[block] = piece
        if half == 0:
            ((_, carried),) = pending.items()
            carry_buf[...] = carried

        @pl.when(grp == 0)
        def _():
            done = columns(chunk, (result_first, result_width))
            branch[:, done] = attended[:, done]
            for step in range(1, groups):
                branch_copy(chunk, half, step).start()

    def gate_of(chunk):
        return jnp.concatenate([gates[0, chunk], gates[1, chunk]], axis=1)

    def finish(chunk):
        cols = columns(chunk)

        @pl.when(grp != 0)
        def _():
            for half in range(2):
                branch_copy(chunk, half, 1).wait_recv()

        relayed = jnp.dot(select[...], branch[:, cols], preferred_element_type=jnp.float32)
        mixed = attended[:, cols].astype(jnp.float32)
        out_ref[:, cols] = (mixed + gate_of(chunk) * relayed).astype(jnp.bfloat16)

    def gradient():
        for step in range(1, groups):
            grad_arrival(step)
        selectors = [selector(which).astype(jnp.bfloat16) for which in range(groups)]

        def one(chunk, carry):
            cols = columns(chunk)
            summed = jnp.zeros((ROWS, CHUNK), jnp.float32)
            for which in range(groups):
                summed = summed + jnp.dot(
                    selectors[which], grads[which, :, cols], preferred_element_type=jnp.float32
                )
            own = grads[0, :, cols].astype(jnp.float32)
            bgrad_ref[:, cols] = (own + gate_of(chunk) * summed).astype(jnp.bfloat16)
            return carry

        lax.fori_loop(0, chunks, one, 0)

    def spread(t, carry):
        on_pass(t, forward)
        relay(t)
        return carry

    lax.fori_loop(0, chunks, spread, 0)
    gate_arrival(core, far_two).wait_recv()
    gate_copies[6].start()

    def body(t, carry):
        @pl.when(t == 2)
        def _():
            for piece in range(n_far):
                gate_arrival(1 - core, piece).wait_recv()
            gradient()

        @pl.when(t < chunks)
        def _():
            arrive(t)
            for half in range(2):
                compute(t, half)

        @pl.when(t >= 2)
        def _():
            finish(t - 2)

        return carry

    lax.fori_loop(0, chunks + 2, body, 0)

    for way, hop, there in tag_sends:

        @pl.when(there)
        def _(way=way, hop=hop):
            tag_copy(way, hop).wait_send()

    def drain(chunk, carry):
        on_crossing(chunk, left_)
        on_own(chunk, left_)
        on_relay(chunk, left_)
        on_pass(chunk, forwarded)
        return carry

    lax.fori_loop(0, chunks, drain, 0)

    for copy in gate_copies:
        copy.wait_send()
    for step in range(1, groups):
        ctrl_copy(step).wait_send()
        grad_copy(step).wait_send()

    @pl.when(grp == 0)
    def _():
        for chunk in range(chunks):
            for half in range(2):
                for step in range(1, groups):
                    branch_copy(chunk, half, step).wait_send()


def local(query_rows, key_rows, value_rows, view_frame, control_row, control_gate, out_grad):
    q, k, v, g = query_rows[0, 0], key_rows[0, 0], value_rows[0, 0], out_grad[0, 0]
    rows, width = q.shape
    chunks = width // CHUNK
    groups = lax.axis_size("grp")
    n_far = lax.axis_size("rep") // 2
    piece = control_gate.shape[0]
    bf16, f32, i32 = jnp.bfloat16, jnp.float32, jnp.int32
    whole = pl.BlockSpec(memory_space=pltpu.VMEM)
    away = pl.BlockSpec(memory_space=pltpu.HBM)
    dma = pltpu.SemaphoreType.DMA
    out, bgrad = pl.pallas_call(
        functools.partial(kernel, chunks),
        out_shape=(
            jax.ShapeDtypeStruct((rows, width), bf16),
            jax.ShapeDtypeStruct((rows, width), bf16),
        ),
        in_specs=[away, away, away, whole, whole, whole, away],
        out_specs=(whole, whole),
        scratch_shapes=[
            pltpu.VMEM((rows, width), bf16),
            pltpu.VMEM((WINDOW, width), bf16),
            pltpu.VMEM((WINDOW, width), bf16),
            pltpu.VMEM((5, 1, rows), i32),
            pltpu.VMEM((groups, 1, rows), i32),
            pltpu.VMEM((2, n_far, 1, piece), f32),
            pltpu.VMEM((groups, rows, width), bf16),
            pltpu.VMEM((rows, WINDOW), f32),
            pltpu.VMEM((rows, rows), bf16),
            pltpu.VMEM((2, 3 * QUARTER, width), bf16),
            pltpu.VMEM((rows, LANES), f32),
            pltpu.VMEM((rows, width), bf16),
            pltpu.VMEM((rows, width), bf16),
            dma((2, 2, chunks, 2)),
            dma((2, 2, chunks, 2, 4)),
            dma((chunks, 2, 4)),
            dma((chunks, 2, 3)),
            dma((chunks, 2, 3)),
            dma((2, 2)),
            dma((2, 2)),
            dma((7,)),
            dma((2, n_far)),
            dma((groups - 1,)),
            dma((groups,)),
            dma((groups - 1,)),
            dma((groups,)),
            dma((chunks, 2, groups - 1)),
            dma((chunks, 2)),
            dma((7,)),
        ],
        compiler_params=pltpu.CompilerParams(
            collective_id=0, has_side_effects=True, vmem_limit_bytes=67_000_000
        ),
    )(
        q,
        k,
        v,
        view_frame.reshape(1, rows),
        control_row.reshape(1, rows),
        control_gate.reshape(1, piece),
        g,
    )
    return out[None, None], bgrad[None]


def solution(mesh):
    seq3 = P("rep", "grp", "seq")
    seq4 = P("rep", "grp", "seq", None)
    return jax.shard_map(
        local,
        mesh=mesh,
        in_specs=(seq4, seq4, seq4, seq3, seq3, P("rep"), seq4),
        out_specs=(seq4, P("rep", "seq", None)),
        check_vma=False,
    )
```

```python
import functools
import math

import jax
import jax.numpy as jnp
from jax import lax
from jax.experimental import pallas as pl
from jax.experimental.pallas import tpu as pltpu
from jax.sharding import PartitionSpec as P

DH = 80
LANES = 128
CHUNK = 640
HEADS_CHUNK = CHUNK // DH
PARTS = (
    (range(0, 5), (0, 384)),
    (range(5, 8), (384, 256)),
)
RUN = 8
QUARTER = 32
ROWS = 128
WINDOW = 5 * ROWS
ABSENT = -1000
MESH = pl.DeviceIdType.MESH
SCALE = math.log2(math.e) / math.sqrt(DH)
OWN, LOWER, UPPER = 2, (1, 0), (3, 4)


def head_spans(head):
    first, last = head * DH, head * DH + DH
    spans = []
    for block in range(first // LANES, (last + LANES - 1) // LANES):
        low = max(first - block * LANES, 0)
        high = min(last - block * LANES, LANES)
        spans.append((block, low, high))
    return spans


def kernel(
    chunks,
    q_hbm,
    k_hbm,
    v_hbm,
    tag_ref,
    ctrl_ref,
    gate_ref,
    grad_hbm,
    out_ref,
    bgrad_ref,
    q_buf,
    k_win,
    v_win,
    tags,
    ctrls,
    gates,
    grads,
    bias,
    select,
    bounce,
    carry_buf,
    attended,
    branch,
    kv_send,
    kv_recv,
    cross_send,
    bounce_recv,
    pass_send,
    tag_send,
    tag_recv,
    gate_send,
    gate_recv,
    spoke_send,
    spoke_recv,
    grad_send,
    grad_recv,
    ctrl_send,
    ctrl_recv,
    br_send,
    br_recv,
    local_sem,
):
    p = lax.axis_index("seq")
    grp = lax.axis_index("grp")
    rep = lax.axis_index("rep")
    length = lax.axis_size("seq")
    groups = lax.axis_size("grp")
    core, far = rep % 2, rep // 2
    n_far = lax.axis_size("rep") // 2
    far_up, far_down, far_two = (far + 1) % n_far, (far + n_far - 1) % n_far, (far + 2) % n_far
    sibling = far * 2 + 1 - core
    has_low, has_high = p >= 1, p <= length - 2
    inner = has_low & has_high
    low2, high2 = p >= 2, p <= length - 3
    place, column, n_columns = p % RUN, p // RUN, length // RUN
    first, last, second, late = place == 0, place == RUN - 1, place == 1, place == RUN - 2
    edge, side = first | last, first | last | second | late
    left, right = column >= 1, column <= n_columns - 2
    side_left, side_right = side & left, side & right
    crosses = (
        (last & right, late & right),
        (first & left, second & left),
    )
    through = (column + 1, n_columns - column)
    passes = ((last & left, late & left), (first & right, second & right))
    passed = (column, n_columns - 1 - column)
    relays = (inner & ~last, inner & ~first)
    hub = place == RUN // 2
    spokes = [offset - RUN // 2 for offset in range(RUN) if offset != RUN // 2]

    barrier = pltpu.get_barrier_semaphore()

    def greet(**where):
        pl.semaphore_signal(barrier, inc=1, device_id=where, device_id_type=MESH)

    @pl.when(has_low)
    def _():
        greet(seq=p - 1)

    @pl.when(has_high)
    def _():
        greet(seq=p + 1)

    @pl.when(low2)
    def _():
        greet(seq=p - 2)

    @pl.when(high2)
    def _():
        greet(seq=p + 2)

    for there, distance in (
        (first, RUN - 1),
        (last, 1 - RUN),
        (first | second, RUN - 2),
        (last | late, 2 - RUN),
        (side_left, -RUN),
        (side_right, RUN),
    ):

        @pl.when(there)
        def _(distance=distance):
            greet(seq=p + distance)

    for step in range(1, groups):
        greet(grp=(grp + step) % groups)

    @pl.when(hub)
    def _():
        greet(rep=sibling)
        greet(rep=far_up * 2 + core)
        greet(rep=far_down * 2 + core)
        for offset in spokes:
            greet(seq=p + offset)

    @pl.when(~hub)
    def _():
        greet(seq=column * RUN + RUN // 2)

    near = groups - 1 + jnp.where(hub, 3 + len(spokes), 1)

    own_rows = pl.ds(OWN * ROWS, ROWS)
    locals_ = [
        pltpu.make_async_copy(q_hbm, q_buf, local_sem.at[0]),
        pltpu.make_async_copy(k_hbm, k_win.at[own_rows, :], local_sem.at[1]),
        pltpu.make_async_copy(v_hbm, v_win.at[own_rows, :], local_sem.at[2]),
        pltpu.make_async_copy(grad_hbm, grads.at[grp], local_sem.at[3]),
        pltpu.make_async_copy(ctrl_ref, ctrls.at[grp], local_sem.at[4]),
        pltpu.make_async_copy(tag_ref, tags.at[OWN], local_sem.at[6]),
    ]
    gate_local = pltpu.make_async_copy(gate_ref, gates.at[core, far], local_sem.at[5])
    for copy in locals_:
        copy.start()

    @pl.when(hub)
    def _():
        gate_local.start()

    def fill(block):
        rows = pl.ds(block * ROWS, ROWS)
        k_win[rows, :] = jnp.zeros((ROWS, k_win.shape[1]), k_win.dtype)
        v_win[rows, :] = jnp.zeros((ROWS, v_win.shape[1]), v_win.dtype)
        tags[block] = jnp.full((1, ROWS), ABSENT, jnp.int32)

    for absent, block in (
        (~has_low, LOWER[0]),
        (~low2, LOWER[1]),
        (~has_high, UPPER[0]),
        (~high2, UPPER[1]),
    ):

        @pl.when(absent)
        def _(block=block):
            fill(block)

    peers = near
    for there in (has_low, has_high, low2, high2, edge, side, side_left, side_right):
        peers = peers + there.astype(jnp.int32)
    pl.semaphore_wait(barrier, peers)

    def columns(chunk, span=(0, CHUNK)):
        start = chunk * CHUNK + span[0]
        if not isinstance(start, int):
            start = pl.multiple_of(start, LANES)
        return pl.ds(start, span[1])

    def kv_copy(way, hop, chunk, part):
        cols = columns(chunk)
        land = (LOWER, UPPER)[way]
        win, hbm = ((k_win, k_hbm), (v_win, v_hbm))[part]
        source = hbm.at[:, cols] if hop == 0 else win.at[pl.ds(land[0] * ROWS, ROWS), cols]
        return pltpu.make_async_remote_copy(
            src_ref=source,
            dst_ref=win.at[pl.ds(land[hop] * ROWS, ROWS), cols],
            send_sem=kv_send.at[way, hop, chunk, part],
            recv_sem=kv_recv.at[way, hop, chunk, part, 0],
            device_id={"seq": p + (1, -1)[way]},
            device_id_type=MESH,
        )

    def cross_copy(way, hop, chunk, part, piece, detour):
        cols = columns(chunk)
        rows = pl.ds(piece * QUARTER, QUARTER)
        if detour:
            target = bounce.at[part, rows, cols]
            arrived, where = bounce_recv.at[chunk, part, piece], p + (RUN, -RUN)[way]
        else:
            block = (LOWER, UPPER)[way][hop]
            target = (k_win, v_win)[part].at[pl.ds(block * ROWS + piece * QUARTER, QUARTER), cols]
            arrived = kv_recv.at[way, hop, chunk, part, piece]
            where = p + (hop + 1, -hop - 1)[way]
        return pltpu.make_async_remote_copy(
            src_ref=(k_hbm, v_hbm)[part].at[rows, cols],
            dst_ref=target,
            send_sem=cross_send.at[chunk, part, piece],
            recv_sem=arrived,
            device_id={"seq": where},
            device_id_type=MESH,
        )

    def pass_copy(way, hop, chunk, part, piece):
        cols = columns(chunk)
        block = (LOWER, UPPER)[way][hop]
        rows = pl.ds(block * ROWS + piece * QUARTER, QUARTER)
        return pltpu.make_async_remote_copy(
            src_ref=bounce.at[part, pl.ds(piece * QUARTER, QUARTER), cols],
            dst_ref=(k_win, v_win)[part].at[rows, cols],
            send_sem=pass_send.at[chunk, part, piece],
            recv_sem=kv_recv.at[way, hop, chunk, part, piece],
            device_id={"seq": p + (1 + hop - RUN, RUN - 1 - hop)[way]},
            device_id_type=MESH,
        )

    def tag_copy(way, hop):
        return pltpu.make_async_remote_copy(
            src_ref=tag_ref,
            dst_ref=tags.at[(LOWER, UPPER)[way][hop]],
            send_sem=tag_send.at[way, hop],
            recv_sem=tag_recv.at[way, hop],
            device_id={"seq": p + (hop + 1, -hop - 1)[way]},
            device_id_type=MESH,
        )

    tag_sends = ((0, 0, has_high), (0, 1, high2), (1, 0, has_low), (1, 1, low2))
    tag_arrivals = ((0, 0, has_low), (0, 1, low2), (1, 0, has_high), (1, 1, high2))

    def on_crossing(chunk, act):
        for way in range(2):
            for hop in range(2):
                for piece in range(4):
                    direct = piece >= through[way]

                    @pl.when(crosses[way][hop] & direct)
                    def _(way=way, hop=hop, piece=piece):
                        for part in range(2):
                            act(cross_copy(way, hop, chunk, part, piece, False))

                    if piece < 3:

                        @pl.when(crosses[way][hop] & ~direct)
                        def _(way=way, hop=hop, piece=piece):
                            for part in range(2):
                                act(cross_copy(way, hop, chunk, part, piece, True))

    def on_own(chunk, act):
        for way, there in ((0, has_high & ~last), (1, has_low & ~first)):

            @pl.when(there)
            def _(way=way):
                for part in range(2):
                    act(kv_copy(way, 0, chunk, part))

    def on_relay(chunk, act):
        for way in range(2):

            @pl.when(relays[way])
            def _(way=way):
                for part in range(2):
                    act(kv_copy(way, 1, chunk, part))

    def on_arrival(way, hop, chunk):
        in_edge = (first, last)[way]

        @pl.when(~in_edge)
        def _():
            for part in range(2):
                kv_copy(way, hop, chunk, part).wait_recv()

        @pl.when(in_edge)
        def _():
            for piece in range(4):
                for part in range(2):
                    cross_copy(way, hop, chunk, part, piece, False).wait_recv()

    def start(copy):
        copy.start()

    def left_(copy):
        copy.wait_send()

    def own_send(chunk):
        on_crossing(chunk, start)
        on_own(chunk, start)

    def relay(chunk):
        for way, here in ((0, has_low), (1, has_high)):

            @pl.when(here)
            def _(way=way):
                on_arrival(way, 0, chunk)

        on_relay(chunk, start)

    def arrive(chunk):
        for way, here in ((0, low2), (1, high2)):

            @pl.when(here)
            def _(way=way):
                on_arrival(way, 1, chunk)

    def on_pass(chunk, act):
        for way in range(2):
            for hop in range(2):
                for piece in range(3):

                    @pl.when(passes[way][hop] & (piece < passed[way]))
                    def _(way=way, hop=hop, piece=piece):
                        for part in range(2):
                            act(way, hop, chunk, part, piece)

    def forward(way, hop, chunk, part, piece):
        cross_copy(way, hop, chunk, part, piece, True).wait_recv()
        pass_copy(way, hop, chunk, part, piece).start()

    def forwarded(way, hop, chunk, part, piece):
        pass_copy(way, hop, chunk, part, piece).wait_send()

    def gate_copy(piece, target, slot, source=None):
        return pltpu.make_async_remote_copy(
            src_ref=gates.at[core, piece] if source is None else source,
            dst_ref=gates.at[core, piece],
            send_sem=gate_send.at[slot],
            recv_sem=gate_recv.at[core, piece],
            device_id={"rep": target},
            device_id_type=MESH,
        )

    to_up, to_down = far_up * 2 + core, far_down * 2 + core
    gate_copies = [
        gate_copy(far, to_up, 0, gate_ref),
        gate_copy(far, to_down, 1, gate_ref),
        gate_copy(far, sibling, 2, gate_ref),
        gate_copy(far_down, to_up, 3),
        gate_copy(far_down, sibling, 4),
        gate_copy(far_up, sibling, 5),
        gate_copy(far_two, sibling, 6),
    ]

    def gate_arrival(which, piece):
        return pltpu.make_async_remote_copy(
            src_ref=gate_ref,
            dst_ref=gates.at[which, piece],
            send_sem=gate_send.at[0],
            recv_sem=gate_recv.at[which, piece],
            device_id={"rep": sibling},
            device_id_type=MESH,
        )

    def spread_copy(number):
        return pltpu.make_async_remote_copy(
            src_ref=gates,
            dst_ref=gates,
            send_sem=spoke_send.at[number],
            recv_sem=spoke_recv,
            device_id={"seq": p + spokes[number]},
            device_id_type=MESH,
        )

    def grad_copy(step):
        return pltpu.make_async_remote_copy(
            src_ref=grad_hbm,
            dst_ref=grads.at[grp],
            send_sem=grad_send.at[step - 1],
            recv_sem=grad_recv.at[grp],
            device_id={"grp": (grp + step) % groups},
            device_id_type=MESH,
        )

    def ctrl_copy(step):
        return pltpu.make_async_remote_copy(
            src_ref=ctrl_ref,
            dst_ref=ctrls.at[grp],
            send_sem=ctrl_send.at[step - 1],
            recv_sem=ctrl_recv.at[grp],
            device_id={"grp": (grp + step) % groups},
            device_id_type=MESH,
        )

    def grad_arrival(step):
        source = (grp + step) % groups
        for src, dst, sem in ((grad_hbm, grads, grad_recv), (ctrl_ref, ctrls, ctrl_recv)):
            pltpu.make_async_remote_copy(
                src_ref=src,
                dst_ref=dst.at[source],
                send_sem=grad_send.at[0],
                recv_sem=sem.at[source],
                device_id={"grp": source},
                device_id_type=MESH,
            ).wait_recv()

    def branch_copy(chunk, half, step):
        cols = columns(chunk, PARTS[half][1])
        return pltpu.make_async_remote_copy(
            src_ref=branch.at[:, cols],
            dst_ref=branch.at[:, cols],
            send_sem=br_send.at[chunk, half, step - 1],
            recv_sem=br_recv.at[chunk, half],
            device_id={"grp": step},
            device_id_type=MESH,
        )

    for way, hop, there in tag_sends:

        @pl.when(there)
        def _(way=way, hop=hop):
            tag_copy(way, hop).start()

    @pl.when(hub)
    def _():
        for copy in gate_copies[:3]:
            copy.start()

    own_send(0)
    own_send(1)
    for step in range(1, groups):
        ctrl_copy(step).start()
        grad_copy(step).start()
    for copy in locals_:
        copy.wait()

    @pl.when(hub)
    def _():
        gate_local.wait()
        gate_arrival(core, far_down).wait_recv()
        gate_copies[3].start()
        gate_copies[4].start()
        gate_arrival(core, far_up).wait_recv()
        gate_copies[5].start()

    own_send(2)

    @pl.when(hub)
    def _():
        gate_arrival(core, far_two).wait_recv()
        gate_copies[6].start()
        for piece in range(n_far):
            gate_arrival(1 - core, piece).wait_recv()
        for number in range(len(spokes)):
            spread_copy(number).start()

    for chunk in range(3, chunks):
        own_send(chunk)

    for way, hop, here in tag_arrivals:

        @pl.when(here)
        def _(way=way, hop=hop):
            tag_copy(way, hop).wait_recv()

    def column_of(row):
        return jnp.broadcast_to(row.astype(jnp.float32), (ROWS, ROWS)).T

    query_tag = column_of(tags[OWN])
    for block in range(5):
        key_tag = jnp.broadcast_to(tags[block].astype(jnp.float32), (ROWS, ROWS))
        gap = jnp.abs(query_tag - key_tag)
        camera = (query_tag >= 20.0) == (key_tag >= 20.0)
        bias[:, block * ROWS : (block + 1) * ROWS] = jnp.where((gap <= 1.0) & camera, 0.0, -1e30)

    def selector(which):
        rows = lax.broadcasted_iota(jnp.int32, (ROWS, ROWS), 0)
        return jnp.where(rows == jnp.broadcast_to(ctrls[which] % ROWS, (ROWS, ROWS)), 1.0, 0.0)

    select[...] = selector(grp).T.astype(jnp.bfloat16)

    lane = lax.broadcasted_iota(jnp.int32, (ROWS, LANES), 1)

    def compute(chunk, half):
        def cols(block, count=1):
            return pl.ds(pl.multiple_of(chunk * CHUNK + block * LANES, LANES), count * LANES)

        heads, (result_first, result_width) = PARTS[half]
        pending = {}
        if half == 1:
            pending[result_first // LANES] = carry_buf[...]
        for head in heads:
            spans = head_spans(head)
            width = len(spans)
            queries = []
            for block, low, high in spans:
                part = q_buf[:, cols(block)]
                if (low, high) != (0, LANES):
                    part = jnp.where((lane >= low) & (lane < high), part, jnp.zeros_like(part))
                queries.append(part)
            query = queries[0] if width == 1 else jnp.concatenate(queries, axis=1)
            where = cols(spans[0][0], width)
            scores = lax.dot_general(
                query, k_win[:, where], (((1,), (1,)), ((), ())), preferred_element_type=jnp.float32
            )
            scores = scores + bias[...]
            largest = jnp.max(scores, axis=1, keepdims=True)
            powers = jnp.exp2((scores - largest) * SCALE)
            totals = jnp.sum(powers, axis=1, keepdims=True)
            weights = (powers * (1.0 / totals)).astype(jnp.bfloat16)
            mixed = jnp.dot(weights, v_win[:, where], preferred_element_type=jnp.float32)
            for number, (block, low, high) in enumerate(spans):
                piece = mixed[:, number * LANES : (number + 1) * LANES]
                if block in pending:
                    piece = jnp.where(lane >= low, piece, pending[block])
                if high == LANES:
                    pending.pop(block, None)
                    attended[:, cols(block)] = piece.astype(jnp.bfloat16)
                else:
                    pending[block] = piece
        if half == 0:
            ((_, carried),) = pending.items()
            carry_buf[...] = carried

        @pl.when(grp == 0)
        def _():
            done = columns(chunk, (result_first, result_width))
            branch[:, done] = attended[:, done]
            for step in range(1, groups):
                branch_copy(chunk, half, step).start()

    def gate_of(chunk):
        return jnp.concatenate([gates[0, chunk], gates[1, chunk]], axis=1)

    def finish(chunk):
        cols = columns(chunk)

        @pl.when(grp != 0)
        def _():
            for half in range(2):
                branch_copy(chunk, half, 1).wait_recv()

        relayed = jnp.dot(select[...], branch[:, cols], preferred_element_type=jnp.float32)
        mixed = attended[:, cols].astype(jnp.float32)
        out_ref[:, cols] = (mixed + gate_of(chunk) * relayed).astype(jnp.bfloat16)

    def gradient():
        for step in range(1, groups):
            grad_arrival(step)
        selectors = [selector(which).astype(jnp.bfloat16) for which in range(groups)]

        def one(chunk, carry):
            cols = columns(chunk)
            summed = jnp.zeros((ROWS, CHUNK), jnp.float32)
            for which in range(groups):
                summed = summed + jnp.dot(
                    selectors[which], grads[which, :, cols], preferred_element_type=jnp.float32
                )
            own = grads[0, :, cols].astype(jnp.float32)
            bgrad_ref[:, cols] = (own + gate_of(chunk) * summed).astype(jnp.bfloat16)
            return carry

        lax.fori_loop(0, chunks, one, 0)

    def spread(t, carry):
        on_pass(t, forward)
        relay(t)
        return carry

    lax.fori_loop(0, chunks, spread, 0)

    def body(t, carry):
        @pl.when(t == 2)
        def _():
            @pl.when(~hub)
            def _():
                spread_copy(0).wait_recv()

            gradient()

        @pl.when(t < chunks)
        def _():
            arrive(t)
            for half in range(2):
                compute(t, half)

        @pl.when(t >= 2)
        def _():
            finish(t - 2)

        return carry

    lax.fori_loop(0, chunks + 2, body, 0)

    for way, hop, there in tag_sends:

        @pl.when(there)
        def _(way=way, hop=hop):
            tag_copy(way, hop).wait_send()

    def drain(chunk, carry):
        on_crossing(chunk, left_)
        on_own(chunk, left_)
        on_relay(chunk, left_)
        on_pass(chunk, forwarded)
        return carry

    lax.fori_loop(0, chunks, drain, 0)

    @pl.when(hub)
    def _():
        for copy in gate_copies:
            copy.wait_send()
        for number in range(len(spokes)):
            spread_copy(number).wait_send()

    for step in range(1, groups):
        ctrl_copy(step).wait_send()
        grad_copy(step).wait_send()

    @pl.when(grp == 0)
    def _():
        for chunk in range(chunks):
            for half in range(2):
                for step in range(1, groups):
                    branch_copy(chunk, half, step).wait_send()


def local(query_rows, key_rows, value_rows, view_frame, control_row, control_gate, out_grad):
    q, k, v, g = query_rows[0, 0], key_rows[0, 0], value_rows[0, 0], out_grad[0, 0]
    rows, width = q.shape
    chunks = width // CHUNK
    groups = lax.axis_size("grp")
    n_far = lax.axis_size("rep") // 2
    piece = control_gate.shape[0]
    bf16, f32, i32 = jnp.bfloat16, jnp.float32, jnp.int32
    whole = pl.BlockSpec(memory_space=pltpu.VMEM)
    away = pl.BlockSpec(memory_space=pltpu.HBM)
    dma = pltpu.SemaphoreType.DMA
    out, bgrad = pl.pallas_call(
        functools.partial(kernel, chunks),
        out_shape=(
            jax.ShapeDtypeStruct((rows, width), bf16),
            jax.ShapeDtypeStruct((rows, width), bf16),
        ),
        in_specs=[away, away, away, whole, whole, whole, away],
        out_specs=(whole, whole),
        scratch_shapes=[
            pltpu.VMEM((rows, width), bf16),
            pltpu.VMEM((WINDOW, width), bf16),
            pltpu.VMEM((WINDOW, width), bf16),
            pltpu.VMEM((5, 1, rows), i32),
            pltpu.VMEM((groups, 1, rows), i32),
            pltpu.VMEM((2, n_far, 1, piece), f32),
            pltpu.VMEM((groups, rows, width), bf16),
            pltpu.VMEM((rows, WINDOW), f32),
            pltpu.VMEM((rows, rows), bf16),
            pltpu.VMEM((2, 3 * QUARTER, width), bf16),
            pltpu.VMEM((rows, LANES), f32),
            pltpu.VMEM((rows, width), bf16),
            pltpu.VMEM((rows, width), bf16),
            dma((2, 2, chunks, 2)),
            dma((2, 2, chunks, 2, 4)),
            dma((chunks, 2, 4)),
            dma((chunks, 2, 3)),
            dma((chunks, 2, 3)),
            dma((2, 2)),
            dma((2, 2)),
            dma((7,)),
            dma((2, n_far)),
            dma((RUN - 1,)),
            dma,
            dma((groups - 1,)),
            dma((groups,)),
            dma((groups - 1,)),
            dma((groups,)),
            dma((chunks, 2, groups - 1)),
            dma((chunks, 2)),
            dma((7,)),
        ],
        compiler_params=pltpu.CompilerParams(
            collective_id=0, has_side_effects=True, vmem_limit_bytes=67_000_000
        ),
    )(
        q,
        k,
        v,
        view_frame.reshape(1, rows),
        control_row.reshape(1, rows),
        control_gate.reshape(1, piece),
        g,
    )
    return out[None, None], bgrad[None]


def solution(mesh):
    seq3 = P("rep", "grp", "seq")
    seq4 = P("rep", "grp", "seq", None)
    return jax.shard_map(
        local,
        mesh=mesh,
        in_specs=(seq4, seq4, seq4, seq3, seq3, P("rep"), seq4),
        out_specs=(seq4, P("rep", "seq", None)),
        check_vma=False,
    )
```
